128 devices in a mesh: dp: 32 (over y, z, core), expert: 4 (over x).
Axes of the slice: x: 4, y: 4, z: 4, core: 2. Of those that a mesh axis runs over, the one named last changes fastest.
Arguments:
- grad_parts: bfloat16 [32, 2048, 6144], P('dp', 'expert')
- bucket_order: int32 [256], replicated, may hold values from 0 to 255, each once
- master: float32 [4, 32, 16, 6144], P('expert', 'dp'), may hold values from -6 to 6
- first_moment: float32 [4, 32, 16, 6144], P('expert', 'dp'), may hold values from -0.6 to 0.6
- second_moment: float32 [4, 32, 16, 6144], P('expert', 'dp'), may hold values from 0.01 to 1
- step_count: int32 [4, 32, 16], P('expert', 'dp'), may hold values from 1 to 8
- max_rms: float32 [1], replicated, may hold values from 0.3 to 1
Outputs:
- new_master: float32 [4, 32, 16, 6144], P('expert', 'dp')
- new_first: float32 [4, 32, 16, 6144], P('expert', 'dp')
- new_second: float32 [4, 32, 16, 6144], P('expert', 'dp')
- new_params: bfloat16 [2048, 6144], P('expert')
The draws below stay inside these ranges and needn't reach their ends.
Inputs may be any that keep to these rules, and one draw needn't show every extreme that they name: bucket_order is a permutation of the 256 buckets.
All inputs are finite; a program needn't handle non-finite values.
Results may differ from the reference program's by a relative error of at most 0.0085.
Values may be sent and summed in bfloat16 or wider, within the bound.
A program may use at most 128 MiB of HBM per device.

```python
import math
import jax
import jax.numpy as jnp
from jax import lax

D = 6144
BROWS = 2
NBK = 256
ROWS = 2048
OWN = 16
N_DP = 32
N_EXPERT = 4


def draw_grad_parts(key, part):
    key_base = jax.random.fold_in(key, 11)
    key_rows = jax.random.fold_in(key, 12)
    base = jax.random.normal(key_base, (N_DP, ROWS, D), jnp.float32)
    ramp = jnp.exp(jnp.log(3.0) * jnp.arange(N_DP, dtype=jnp.float32) / max(N_DP - 1, 1)).reshape(N_DP, 1, 1)
    row_scale = jnp.exp(jax.random.uniform(key_rows, (1, ROWS, 1), jnp.float32) * jnp.log(10.0))
    return (base * row_scale * ramp).astype(jnp.bfloat16)


def set_ends(array, stream_key, smallest, top_value):
    place = [jax.random.randint(jax.random.fold_in(stream_key, axis), (), 0, length) for axis, length in enumerate(array.shape)]
    longest = array.shape.index(max(array.shape))
    neighbour = place[:longest] + [(place[longest] + 1) % array.shape[longest]] + place[longest + 1:]
    return array.at[tuple(place)].set(smallest).at[tuple(neighbour)].set(top_value)


def block_scale(key, dims, cuts, smallest, high):
    gain = 1.0
    for dim, shards_of in cuts:
        draws = jax.random.uniform(jax.random.fold_in(jax.random.fold_in(key, 6), dim), (shards_of,), jnp.float32, smallest / len(cuts), high / len(cuts))
        gain = gain * jnp.repeat(jnp.exp(draws), dims[dim] // shards_of).reshape((-1,) + (1,) * (len(dims) - 1 - dim))
    return gain


def noise(key, dims, width, bound, split=(), held_as=jnp.bfloat16):
    level = block_scale(key, dims, split, -0.22, 0.18) if split else 1.0
    result = jax.random.normal(key, dims, jnp.float32) * width * level
    return jnp.minimum(jnp.maximum(result, -bound), bound).astype(held_as)


def setup_inputs(seed: int = 0) -> dict:
    streams_of = jax.random.split(jax.random.key(seed), 8)
    return {
        "grad_parts": draw_grad_parts(jax.random.fold_in(streams_of[7], 71), 0),
        "bucket_order": jax.random.permutation(streams_of[1], NBK).astype(jnp.int32),
        "master": noise(streams_of[2], (N_EXPERT, N_DP, OWN, D), 1.0, 6.0, ((0, 4), (1, 32)), jnp.float32),
        "first_moment": noise(streams_of[3], (N_EXPERT, N_DP, OWN, D), 0.1, 0.6, ((0, 4), (1, 32)), jnp.float32),
        "second_moment": jnp.clip(jnp.exp(math.log(1.0) - 4.6051702 * jax.random.uniform(streams_of[4], (N_EXPERT, N_DP, OWN, D), jnp.float32) ** block_scale(streams_of[4], (N_EXPERT, N_DP, OWN, D), ((0, 4), (1, 32)), -0.2, 0.2)), 0.01, 1.0),
        "step_count": set_ends(jax.random.randint(streams_of[5], (N_EXPERT, N_DP, OWN), 1, 9), jax.random.fold_in(streams_of[5], 1), 1, 8).astype(jnp.int32),
        "max_rms": jnp.clip(jax.random.uniform(streams_of[6], (1,), jnp.float32, 0.3, 1.0), 0.3, 1.0),
    }


def reference(grad_parts, bucket_order, master, first_moment, second_moment, step_count, max_rms):

    def accumulate(index, running):
        piece = lax.dynamic_index_in_dim(grad_parts, index, 0, keepdims=False)
        return running + piece.astype(jnp.float32)
    grad_total = lax.fori_loop(0, N_DP, accumulate, jnp.zeros((ROWS, D), jnp.float32))
    square_sum = jnp.sum(grad_total * grad_total)
    entries = float(ROWS * D)
    clip_factor = jnp.minimum(1.0, max_rms[0] / jnp.sqrt(square_sum / entries + 1e-06))
    blocks = grad_total.reshape(N_EXPERT, NBK, BROWS, D)[:, bucket_order]
    slotted = blocks.reshape(N_EXPERT, N_DP, OWN, D)
    clipped = clip_factor * slotted
    new_first = 0.9 * first_moment + 0.1 * clipped
    new_second = 0.95 * second_moment + 0.05 * clipped * clipped
    step_float = step_count.astype(jnp.float32)[..., None]
    first_fix = 1.0 - jnp.power(jnp.float32(0.9), step_float)
    second_fix = 1.0 - jnp.power(jnp.float32(0.95), step_float)
    ratio = new_first / first_fix / (jnp.sqrt(new_second / second_fix) + 1e-08)
    new_master = master - 0.1 * (ratio + 0.1 * master)
    rounded = new_master.astype(jnp.bfloat16).reshape(N_EXPERT, NBK, BROWS, D)
    placed = jnp.zeros_like(rounded).at[:, bucket_order].set(rounded)
    return (new_master, new_first, new_second, placed.reshape(ROWS, D))
```

```python
import functools

import jax
import jax.numpy as jnp
from jax import lax
from jax.experimental import pallas as pl
from jax.experimental.pallas import tpu as pltpu
from jax.sharding import Mesh
from jax.sharding import PartitionSpec as P

MESH = pl.DeviceIdType.MESH
BF16, F32 = jnp.bfloat16, jnp.float32
N = 4
WR = 512
WG = 1024
TILE = 256


def away(axis, by, n=N):
    return lax.rem(lax.axis_index(axis) + by, n)


def main_kernel(
    sizes, order, steps, max_rms, grad, master, first, second,
    out, new_master, new_first, new_second,
    own, sib, sb, hop, fin, s2, r2, tot, gsum, slots, perm, perm_t, st, fix, sq, s1, s2nd,
    load_sem, pair_sem, hop_sem, fin_sem, r2_sem, tot_sem, st_sem, x_sem, yz_sem, p1_sem, p2_sem, fwd_sem, half_sem,
):
    rows, width, nr, ng, entries = sizes
    my, mz, mc, mx = (lax.axis_index(a) for a in "yzcx")
    half = width // 2
    coords = {"y": my, "z": mz}

    def axes(block):
        return ("y", "z") if block % 2 == 0 else ("z", "y")

    def remote(src, dst, sems, at, where):
        return pltpu.make_async_remote_copy(
            src_ref=src, dst_ref=dst, send_sem=sems.at[(0, *at)], recv_sem=sems.at[(1, *at)],
            device_id=where, device_id_type=MESH,
        )

    sent = []

    def start(copies):
        for c in copies:
            c.start()
        sent.extend(copies)
        return copies

    def arrived(copies):
        for c in copies:
            c.wait_recv()

    def load(k):
        cols = pl.ds(pl.multiple_of(mc * half + k * WR, WR), WR)
        return pltpu.make_async_copy(grad.at[0, :, cols], own.at[k], load_sem.at[k])

    loads = [load(k) for k in range(nr)]
    states = [
        pltpu.make_async_copy(a.at[0, 0], st.at[i], st_sem.at[i])
        for i, a in enumerate((master, first, second))
    ]
    for c in loads:
        c.start()
    for c in states:
        c.start()

    sibling = {"c": 1 - mc}
    group_x = [(i, j) for i in range(N) for j in range(2) if i or j]
    group_yz = [(i, j) for i in range(N) for j in range(N) if i or j]
    peers_x = [{"x": away("x", i), "c": away("c", j, 2)} for i, j in group_x]
    peers_yz = [{"y": away("y", i), "z": away("z", j)} for i, j in group_yz]
    barrier = pltpu.get_barrier_semaphore()
    for peer in [*peers_x, *peers_yz]:
        pl.semaphore_signal(barrier, inc=1, device_id=peer, device_id_type=MESH)

    def fill(t, _):
        i = lax.broadcasted_iota(jnp.int32, (16, rows), 0)
        picked = jnp.zeros((16, rows), jnp.int32)
        for b in range(8):
            picked = jnp.where(i // 2 == b, order[t * 8 + b] * 2, picked)
        hit = lax.broadcasted_iota(jnp.int32, (16, rows), 1) == picked + i % 2
        perm[pl.ds(pl.multiple_of(t * 16, 16), 16), :] = jnp.where(hit, 1.0, 0.0).astype(BF16)
        return 0

    lax.fori_loop(0, rows // 16, fill, 0)
    pl.semaphore_wait(barrier, len(peers_x) + len(peers_yz))

    def pair(k):
        cols = pl.ds(pl.multiple_of((1 - mc) * half + k * WR, WR), WR)
        return remote(grad.at[0, :, cols], sib.at[k], pair_sem, (k,), sibling)

    pairs = start([pair(k) for k in range(nr)])

    def pick_rows(k):
        loads[k].wait()
        arrived([pairs[k]])
        for t in range(WR // TILE):
            cols = pl.ds(t * TILE, TILE)
            both = own[k, :, cols].astype(F32) + sib[k, :, cols].astype(F32)
            moved = jnp.dot(perm[...], both.astype(BF16), preferred_element_type=F32)
            moved = moved.astype(BF16).reshape(N, N, 32, TILE)
            for i in range(N):
                for j in range(N):
                    at = (i, j) if k % 2 == 0 else (j, i)
                    sb[k, at[0], at[1], :, cols] = moved[i, j]

    def beside(axis):
        return coords[axis], away(axis, 1), away(axis, 2), away(axis, 3)

    lo, hi = pl.ds(0, 2), pl.ds(2, 2)

    def first_hops(k):
        a = axes(k)[0]
        _, up, far, down = beside(a)
        hops = [
            remote(sb.at[k, far, lo], hop.at[k, 0], hop_sem, (k, 0), {a: up}),
            remote(sb.at[k, far, hi], hop.at[k, 1], hop_sem, (k, 1), {a: down}),
        ]
        plain = [
            remote(sb.at[k, up, hi], fin.at[k, 0, hi], fin_sem, (k, 0), {a: up}),
            remote(sb.at[k, down, lo], fin.at[k, 1, lo], fin_sem, (k, 1), {a: down}),
        ]
        return start(hops), start(plain)

    def add_into(k, to, j0, slot):
        def body(i, _):
            j, r = i // 2, pl.ds(pl.multiple_of((i % 2) * 16, 16), 16)
            total = sb[k, to, j0 + j, r, :].astype(F32) + hop[k, slot, j, r, :].astype(F32)
            sb[k, to, j0 + j, r, :] = total.astype(BF16)
            return 0

        lax.fori_loop(0, 4, body, 0)

    def second_hops(k, hops):
        a = axes(k)[0]
        _, up, _, down = beside(a)
        arrived([hops[0]])
        add_into(k, up, 0, 0)
        one = remote(sb.at[k, up, lo], fin.at[k, 0, lo], fin_sem, (k, 2), {a: up})
        start([one])
        arrived([hops[1]])
        add_into(k, down, 2, 1)
        two = remote(sb.at[k, down, hi], fin.at[k, 1, hi], fin_sem, (k, 3), {a: down})
        start([two])
        return [one, two]

    def sum3(k, me, j, r):
        return sb[k, me, j, r, :].astype(F32) + fin[k, 0, j, r, :].astype(F32) + fin[k, 1, j, r, :].astype(F32)

    def across(k, waits):
        a, b = axes(k)
        me = coords[a]
        arrived(waits)
        copies = []
        for d in (2, 1, 3):
            j = away(b, d)

            def body(i, _, j=j, d=d):
                r = pl.ds(pl.multiple_of(i * 16, 16), 16)
                s2[k, d - 1, r, :] = sum3(k, me, j, r).astype(BF16)
                return 0

            lax.fori_loop(0, 2, body, 0)
            copies += start([remote(s2.at[k, d - 1], r2.at[k, d - 1], r2_sem, (k, d - 1), {b: j})])
        return copies

    def finish(k, waits):
        a, b = axes(k)
        me, mj = coords[a], coords[b]
        arrived(waits)
        cols = pl.ds(pl.multiple_of(mc * half + k * WR, WR), WR)
        for i in range(2):
            r = pl.ds(i * 16, 16)
            total = sum3(k, me, mj, r)
            for d in range(3):
                total = total + r2[k, d, r, :].astype(F32)
            tot[k, i] = total
            square = total * total
            folded = square[:, :128]
            for t in range(1, WR // 128):
                folded = folded + square[:, t * 128 : (t + 1) * 128]
            sq[...] += folded[:8] + folded[8:]
        gsum[:, cols] = tot[k, mc]
        return start([remote(tot.at[k, 1 - mc], gsum.at[:, cols], tot_sem, (k,), sibling)])

    sq[...] = jnp.zeros_like(sq)
    hops, plain, second_half, sums, shared = {}, {}, {}, {}, []
    for t in range(nr + 3):
        if t < nr:
            pick_rows(t)
            hops[t], plain[t] = first_hops(t)
        if 0 <= t - 1 < nr:
            second_half[t - 1] = second_hops(t - 1, hops[t - 1])
        if 0 <= t - 2 < nr:
            sums[t - 2] = across(t - 2, plain[t - 2] + second_half[t - 2])
        if 0 <= t - 3 < nr:
            shared += finish(t - 3, sums[t - 3])

    mine_x, mine_yz = mx * 2 + mc, my * N + mz
    s1[mine_x] = sq[...]
    across_x = start([
        remote(sq, s1.at[mine_x], x_sem, (n,), peer) for n, peer in enumerate(peers_x)
    ])

    def flip(t, _):
        r = pl.ds(pl.multiple_of(t * 128, 128), 128)
        i = lax.broadcasted_iota(jnp.int32, (128, rows), 0) + t * 128
        eye = jnp.where(i == lax.broadcasted_iota(jnp.int32, (128, rows), 1), 1.0, 0.0).astype(BF16)
        perm_t[r, :] = lax.dot_general(
            eye, perm[...], (((1,), (1,)), ((), ())), preferred_element_type=F32
        ).astype(BF16)
        return 0

    lax.fori_loop(0, rows // 128, flip, 0)
    lane_row = lax.broadcasted_iota(jnp.int32, (16, 128), 0)
    count = jnp.zeros((16, 128), jnp.int32)
    for i in range(16):
        count = jnp.where(lane_row == i, steps[0, 0, i], count)
    count = count.astype(F32)
    fix[0] = 1.0 - jnp.power(jnp.full((16, 128), 0.9, F32), count)
    fix[1] = 1.0 - jnp.power(jnp.full((16, 128), 0.95, F32), count)
    for c in states:
        c.wait()

    arrived(across_x)
    part = s1[0]
    for i in range(1, 2 * N):
        part = part + s1[i]
    s2nd[mine_yz] = part
    mine = s2nd.at[mine_yz]
    across_yz = start([remote(mine, mine, yz_sem, (n,), peer) for n, peer in enumerate(peers_yz)])
    arrived(shared)
    arrived(across_yz)
    part = s2nd[0]
    for i in range(1, N * N):
        part = part + s2nd[i]
    square_sum = jnp.sum(jnp.sum(part, axis=1, keepdims=True), axis=0, keepdims=True)
    clip = jnp.minimum(1.0, max_rms[0] / jnp.sqrt(square_sum / entries + 1e-06))

    def update(k):
        def body(t, _):
            cols = pl.ds(pl.multiple_of(k * WG + t * 128, 128), 128)
            clipped = clip * gsum[:, cols]
            moment = 0.9 * st[1, :, cols] + 0.1 * clipped
            variance = 0.95 * st[2, :, cols] + 0.05 * clipped * clipped
            ratio = moment / fix[0] / (jnp.sqrt(variance / fix[1]) + 1e-08)
            old = st[0, :, cols]
            fresh = old - 0.1 * (ratio + 0.1 * old)
            new_master[0, 0, :, cols] = fresh
            new_first[0, 0, :, cols] = moment
            new_second[0, 0, :, cols] = variance
            slots[my, mz, mc, :, cols] = fresh.astype(BF16)
            return 0

        lax.fori_loop(0, WG // 128, body, 0)
        cols = pl.ds(k * WG, WG)
        a = axes(k)[0]
        mine = slots.at[my, mz, mc, :, cols]
        return start([remote(mine, mine, p1_sem, (k, d - 1), {a: away(a, d)}) for d in (2, 1, 3)])

    def row(k, at, part):
        cols = pl.ds(k * WG, WG)
        if k % 2 == 0:
            return slots.at[part, at, mc, :, cols]
        return slots.at[at, part, mc, :, cols]

    def spread(k, waits):
        arrived(waits)
        b = axes(k)[1]
        me, up, _, down = beside(b)
        mine = row(k, me, pl.ds(0, N))
        return start([
            remote(mine, mine, p2_sem, (k, 0), {b: up}),
            remote(mine, mine, p2_sem, (k, 1), {b: down}),
        ])

    def forward(k, waits):
        b = axes(k)[1]
        _, up, _, down = beside(b)
        arrived(waits[:1])
        one, two = row(k, down, lo), row(k, up, hi)
        copies = start([remote(one, one, fwd_sem, (k, 0), {b: up})])
        arrived(waits[1:])
        return copies + start([remote(two, two, fwd_sem, (k, 1), {b: down})])

    def to_sibling(k, waits):
        arrived(waits)
        block = slots.at[:, :, mc, :, pl.ds(k * WG, WG)]
        return start([remote(block, block, half_sem, (k,), sibling)])

    def put_back(k, waits):
        arrived(waits)
        for t in range(WG // TILE):
            cols = pl.ds(k * WG + t * TILE, TILE)
            block = slots[:, :, :, :, cols].reshape(rows, TILE)
            out[:, cols] = jnp.dot(perm_t[...], block, preferred_element_type=F32).astype(BF16)

    ups = [update(k) for k in range(ng)]
    across_b, forwards, halves = {}, {}, {}
    for t in range(ng + 3):
        if t < ng:
            across_b[t] = spread(t, ups[t])
        if 0 <= t - 1 < ng:
            forwards[t - 1] = forward(t - 1, across_b[t - 1])
        if 0 <= t - 2 < ng:
            halves[t - 2] = to_sibling(t - 2, forwards[t - 2])
        if 0 <= t - 3 < ng:
            put_back(t - 3, halves[t - 3])
    for c in sent:
        c.wait_send()


def write_kernel(*refs):
    n = (len(refs) - 1) // 2
    copies = [
        pltpu.make_async_copy(refs[i], refs[n + i], refs[2 * n].at[i]) for i in range(n)
    ]
    for c in copies:
        c.start()
    for c in copies:
        c.wait()


def shards(grad_parts, bucket_order, master, first_moment, second_moment, step_count, max_rms):
    _, rows, width = grad_parts.shape
    own_rows = master.shape[2]
    nr, ng = width // 2 // WR, width // WG
    entries = float(rows * width * lax.axis_size("x"))
    dma = pltpu.SemaphoreType.DMA
    anywhere = pl.BlockSpec(memory_space=pl.ANY)
    smem = pl.BlockSpec(memory_space=pltpu.SMEM)
    vmem = pl.BlockSpec(memory_space=pltpu.VMEM)
    state = pltpu.VMEM(master.shape, F32)
    results = pl.pallas_call(
        functools.partial(main_kernel, (rows, width, nr, ng, entries)),
        out_shape=(pltpu.VMEM((rows, width), BF16), state, state, state),
        in_specs=[smem] * 3 + [pl.BlockSpec(memory_space=pltpu.HBM)] * 4,
        out_specs=[vmem] * 4,
        scratch_shapes=[
            pltpu.VMEM((nr, rows, WR), BF16),
            pltpu.VMEM((nr, rows, WR), BF16),
            pltpu.VMEM((nr, N, N, 32, WR), BF16),
            pltpu.VMEM((nr, 2, 2, 32, WR), BF16),
            pltpu.VMEM((nr, 2, N, 32, WR), BF16),
            pltpu.VMEM((nr, 3, 32, WR), BF16),
            pltpu.VMEM((nr, 3, 32, WR), BF16),
            pltpu.VMEM((nr, 2, 16, WR), F32),
            pltpu.VMEM((own_rows, width), F32),
            pltpu.VMEM((N, N, 2, own_rows, width), BF16),
            pltpu.VMEM((rows, rows), BF16),
            pltpu.VMEM((rows, rows), BF16),
            pltpu.VMEM((3, own_rows, width), F32),
            pltpu.VMEM((2, own_rows, 128), F32),
            pltpu.VMEM((8, 128), F32),
            pltpu.VMEM((2 * N, 8, 128), F32),
            pltpu.VMEM((N * N, 8, 128), F32),
            dma((nr,)),
            dma((2, nr)),
            dma((2, nr, 2)),
            dma((2, nr, 4)),
            dma((2, nr, 3)),
            dma((2, nr)),
            dma((3,)),
            dma((2, 7)),
            dma((2, 15)),
            dma((2, ng, 3)),
            dma((2, ng, 2)),
            dma((2, ng, 2)),
            dma((2, ng)),
        ],
        compiler_params=pltpu.CompilerParams(
            collective_id=0, has_side_effects=True, vmem_limit_bytes=48 << 20
        ),
    )(bucket_order, step_count, max_rms, grad_parts, master, first_moment, second_moment)
    fresh, *moved = pl.pallas_call(
        write_kernel,
        out_shape=[jax.ShapeDtypeStruct(r.shape, r.dtype) for r in results],
        in_specs=[anywhere] * 4,
        out_specs=[pl.BlockSpec(memory_space=pltpu.HBM)] * 4,
        scratch_shapes=[dma((4,))],
    )(*results)
    return (*moved, fresh)


def solution(mesh):
    dp = ("y", "z", "c")
    finer = Mesh(mesh.devices.reshape(N, N, 2, mesh.shape["expert"]), (*dp, "x"))
    state = P("x", dp, None, None)
    return jax.shard_map(
        shards,
        mesh=finer,
        in_specs=(P(dp, "x", None), P(), state, state, state, P("x", dp, None), P()),
        out_specs=(state, state, state, P("x", None)),
        check_vma=False,
    )
```

```python
import functools

import jax
import jax.numpy as jnp
from jax import lax
from jax.experimental import pallas as pl
from jax.experimental.pallas import tpu as pltpu
from jax.sharding import Mesh
from jax.sharding import PartitionSpec as P

MESH = pl.DeviceIdType.MESH
BF16, F32 = jnp.bfloat16, jnp.float32
N = 4
WR = 512
WG = 1024
TILE = 256


def away(axis, by, n=N):
    return lax.rem(lax.axis_index(axis) + by, n)


def main_kernel(
    sizes, order, steps, max_rms, grad, master, first, second,
    out, new_master, new_first, new_second,
    own, sib, sb, hop, fin, s2, r2, tot, gsum, slots, perm, perm_t, st, fix, sq, s1, s2nd,
    load_sem, pair_sem, hop_sem, fin_sem, r2_sem, tot_sem, st_sem, x_sem, yz_sem, p1_sem, p2_sem, fwd_sem, half_sem,
):
    rows, width, nr, ng, entries = sizes
    my, mz, mc, mx = (lax.axis_index(a) for a in "yzcx")
    half = width // 2
    coords = {"y": my, "z": mz}

    def axes(block):
        return ("y", "z") if block % 2 == 0 else ("z", "y")

    def remote(src, dst, sems, at, where):
        return pltpu.make_async_remote_copy(
            src_ref=src, dst_ref=dst, send_sem=sems.at[(0, *at)], recv_sem=sems.at[(1, *at)],
            device_id=where, device_id_type=MESH,
        )

    sent = []

    def start(copies):
        for c in copies:
            c.start()
        sent.extend(copies)
        return copies

    def arrived(copies):
        for c in copies:
            c.wait_recv()

    def load(k):
        cols = pl.ds(pl.multiple_of(mc * half + k * WR, WR), WR)
        return pltpu.make_async_copy(grad.at[0, :, cols], own.at[k], load_sem.at[k])

    loads = [load(k) for k in range(nr)]
    states = [
        pltpu.make_async_copy(a.at[0, 0], st.at[i], st_sem.at[i])
        for i, a in enumerate((master, first, second))
    ]
    for c in loads:
        c.start()
    for c in states:
        c.start()

    sibling = {"c": 1 - mc}
    group_x = [(i, j) for i in range(N) for j in range(2) if i or j]
    group_yz = [(i, j) for i in range(N) for j in range(N) if i or j]
    peers_x = [{"x": away("x", i), "c": away("c", j, 2)} for i, j in group_x]
    peers_yz = [{"y": away("y", i), "z": away("z", j)} for i, j in group_yz]
    barrier = pltpu.get_barrier_semaphore()
    for peer in [*peers_x, *peers_yz]:
        pl.semaphore_signal(barrier, inc=1, device_id=peer, device_id_type=MESH)

    def fill(t, _):
        i = lax.broadcasted_iota(jnp.int32, (16, rows), 0)
        picked = jnp.zeros((16, rows), jnp.int32)
        for b in range(8):
            picked = jnp.where(i // 2 == b, order[t * 8 + b] * 2, picked)
        hit = lax.broadcasted_iota(jnp.int32, (16, rows), 1) == picked + i % 2
        perm[pl.ds(pl.multiple_of(t * 16, 16), 16), :] = jnp.where(hit, 1.0, 0.0).astype(BF16)
        return 0

    lax.fori_loop(0, rows // 16, fill, 0)
    pl.semaphore_wait(barrier, len(peers_x) + len(peers_yz))

    def pair(k):
        cols = pl.ds(pl.multiple_of((1 - mc) * half + k * WR, WR), WR)
        return remote(grad.at[0, :, cols], sib.at[k], pair_sem, (k,), sibling)

    pairs = start([pair(k) for k in range(nr)])

    def pick_rows(k):
        loads[k].wait()
        arrived([pairs[k]])
        for t in range(WR // TILE):
            cols = pl.ds(t * TILE, TILE)
            both = own[k, :, cols].astype(F32) + sib[k, :, cols].astype(F32)
            moved = jnp.dot(perm[...], both.astype(BF16), preferred_element_type=F32)
            moved = moved.astype(BF16).reshape(N, N, 32, TILE)
            for i in range(N):
                for j in range(N):
                    at = (i, j) if k % 2 == 0 else (j, i)
                    sb[k, at[0], at[1], :, cols] = moved[i, j]

    def beside(axis):
        return coords[axis], away(axis, 1), away(axis, 2), away(axis, 3)

    lo, hi = pl.ds(0, 2), pl.ds(2, 2)

    def first_hops(k):
        a = axes(k)[0]
        _, up, far, down = beside(a)
        hops = [
            remote(sb.at[k, far, lo], hop.at[k, 0], hop_sem, (k, 0), {a: up}),
            remote(sb.at[k, far, hi], hop.at[k, 1], hop_sem, (k, 1), {a: down}),
        ]
        plain = [
            remote(sb.at[k, up, hi], fin.at[k, 0, hi], fin_sem, (k, 0), {a: up}),
            remote(sb.at[k, down, lo], fin.at[k, 1, lo], fin_sem, (k, 1), {a: down}),
        ]
        return start(hops), start(plain)

    def add_into(k, to, j0, slot):
        def body(i, _):
            j, r = i // 2, pl.ds(pl.multiple_of((i % 2) * 16, 16), 16)
            total = sb[k, to, j0 + j, r, :].astype(F32) + hop[k, slot, j, r, :].astype(F32)
            sb[k, to, j0 + j, r, :] = total.astype(BF16)
            return 0

        lax.fori_loop(0, 4, body, 0)

    def second_hops(k, hops):
        a = axes(k)[0]
        _, up, _, down = beside(a)
        arrived([hops[0]])
        add_into(k, up, 0, 0)
        one = remote(sb.at[k, up, lo], fin.at[k, 0, lo], fin_sem, (k, 2), {a: up})
        start([one])
        arrived([hops[1]])
        add_into(k, down, 2, 1)
        two = remote(sb.at[k, down, hi], fin.at[k, 1, hi], fin_sem, (k, 3), {a: down})
        start([two])
        return [one, two]

    def sum3(k, me, j, r):
        return sb[k, me, j, r, :].astype(F32) + fin[k, 0, j, r, :].astype(F32) + fin[k, 1, j, r, :].astype(F32)

    def across(k, waits):
        a, b = axes(k)
        me = coords[a]
        arrived(waits)
        copies = []
        for d in (2, 1, 3):
            j = away(b, d)

            def body(i, _, j=j, d=d):
                r = pl.ds(pl.multiple_of(i * 16, 16), 16)
                s2[k, d - 1, r, :] = sum3(k, me, j, r).astype(BF16)
                return 0

            lax.fori_loop(0, 2, body, 0)
            copies += start([remote(s2.at[k, d - 1], r2.at[k, d - 1], r2_sem, (k, d - 1), {b: j})])
        return copies

    def finish(k, waits):
        a, b = axes(k)
        me, mj = coords[a], coords[b]
        arrived(waits)
        cols = pl.ds(pl.multiple_of(mc * half + k * WR, WR), WR)
        for i in range(2):
            r = pl.ds(i * 16, 16)
            total = sum3(k, me, mj, r)
            for d in range(3):
                total = total + r2[k, d, r, :].astype(F32)
            tot[k, i] = total
            square = total * total
            folded = square[:, :128]
            for t in range(1, WR // 128):
                folded = folded + square[:, t * 128 : (t + 1) * 128]
            sq[...] += folded[:8] + folded[8:]
        gsum[:, cols] = tot[k, mc]
        return start([remote(tot.at[k, 1 - mc], gsum.at[:, cols], tot_sem, (k,), sibling)])

    sq[...] = jnp.zeros_like(sq)
    hops, plain, second_half, sums, shared = {}, {}, {}, {}, []
    for t in range(nr + 3):
        if t < nr:
            pick_rows(t)
            hops[t], plain[t] = first_hops(t)
        if 0 <= t - 1 < nr:
            second_half[t - 1] = second_hops(t - 1, hops[t - 1])
        if 0 <= t - 2 < nr:
            sums[t - 2] = across(t - 2, plain[t - 2] + second_half[t - 2])
        if 0 <= t - 3 < nr:
            shared += finish(t - 3, sums[t - 3])

    mine_x, mine_yz = mx * 2 + mc, my * N + mz
    s1[mine_x] = sq[...]
    across_x = start([
        remote(sq, s1.at[mine_x], x_sem, (n,), peer) for n, peer in enumerate(peers_x)
    ])

    def flip(t, _):
        r = pl.ds(pl.multiple_of(t * 128, 128), 128)
        i = lax.broadcasted_iota(jnp.int32, (128, rows), 0) + t * 128
        eye = jnp.where(i == lax.broadcasted_iota(jnp.int32, (128, rows), 1), 1.0, 0.0).astype(BF16)
        perm_t[r, :] = lax.dot_general(
            eye, perm[...], (((1,), (1,)), ((), ())), preferred_element_type=F32
        ).astype(BF16)
        return 0

    lax.fori_loop(0, rows // 128, flip, 0)
    lane_row = lax.broadcasted_iota(jnp.int32, (16, 128), 0)
    count = jnp.zeros((16, 128), jnp.int32)
    for i in range(16):
        count = jnp.where(lane_row == i, steps[0, 0, i], count)
    count = count.astype(F32)
    fix[0] = 1.0 - jnp.power(jnp.full((16, 128), 0.9, F32), count)
    fix[1] = 1.0 - jnp.power(jnp.full((16, 128), 0.95, F32), count)
    for c in states:
        c.wait()

    arrived(across_x)
    part = s1[0]
    for i in range(1, 2 * N):
        part = part + s1[i]
    s2nd[mine_yz] = part
    mine = s2nd.at[mine_yz]
    across_yz = start([remote(mine, mine, yz_sem, (n,), peer) for n, peer in enumerate(peers_yz)])
    arrived(shared)
    arrived(across_yz)
    part = s2nd[0]
    for i in range(1, N * N):
        part = part + s2nd[i]
    square_sum = jnp.sum(jnp.sum(part, axis=1, keepdims=True), axis=0, keepdims=True)
    clip = jnp.minimum(1.0, max_rms[0] / jnp.sqrt(square_sum / entries + 1e-06))

    def update(k):
        def body(t, _):
            cols = pl.ds(pl.multiple_of(k * WG + t * 128, 128), 128)
            clipped = clip * gsum[:, cols]
            moment = 0.9 * st[1, :, cols] + 0.1 * clipped
            variance = 0.95 * st[2, :, cols] + 0.05 * clipped * clipped
            ratio = moment / fix[0] / (jnp.sqrt(variance / fix[1]) + 1e-08)
            old = st[0, :, cols]
            fresh = old - 0.1 * (ratio + 0.1 * old)
            new_master[0, 0, :, cols] = fresh
            new_first[0, 0, :, cols] = moment
            new_second[0, 0, :, cols] = variance
            slots[my, mz, mc, :, cols] = fresh.astype(BF16)
            return 0

        lax.fori_loop(0, WG // 128, body, 0)
        cols = pl.ds(k * WG, WG)
        a = axes(k)[0]
        mine = slots.at[my, mz, mc, :, cols]
        return start([remote(mine, mine, p1_sem, (k, d - 1), {a: away(a, d)}) for d in (2, 1, 3)])

    def row(k, at, part):
        cols = pl.ds(k * WG, WG)
        if k % 2 == 0:
            return slots.at[part, at, mc, :, cols]
        return slots.at[at, part, mc, :, cols]

    def spread(k, waits):
        arrived(waits)
        b = axes(k)[1]
        me, up, _, down = beside(b)
        mine = row(k, me, pl.ds(0, N))
        return start([
            remote(mine, mine, p2_sem, (k, 0), {b: up}),
            remote(mine, mine, p2_sem, (k, 1), {b: down}),
        ])

    def forward(k, waits):
        b = axes(k)[1]
        _, up, _, down = beside(b)
        arrived(waits[:1])
        one, two = row(k, down, lo), row(k, up, hi)
        copies = start([remote(one, one, fwd_sem, (k, 0), {b: up})])
        arrived(waits[1:])
        return copies + start([remote(two, two, fwd_sem, (k, 1), {b: down})])

    def to_sibling(k, waits):
        arrived(waits)
        block = slots.at[:, :, mc, :, pl.ds(k * WG, WG)]
        return start([remote(block, block, half_sem, (k,), sibling)])

    def put_back(k, waits):
        arrived(waits)
        for t in range(WG // TILE):
            cols = pl.ds(k * WG + t * TILE, TILE)
            block = slots[:, :, :, :, cols].reshape(rows, TILE)
            out[:, cols] = jnp.dot(perm_t[...], block, preferred_element_type=F32).astype(BF16)

    ups = [update(k) for k in range(ng)]
    across_b, forwards, halves = {}, {}, {}
    for t in range(ng + 3):
        if t < ng:
            across_b[t] = spread(t, ups[t])
        if 0 <= t - 1 < ng:
            forwards[t - 1] = forward(t - 1, across_b[t - 1])
        if 0 <= t - 2 < ng:
            halves[t - 2] = to_sibling(t - 2, forwards[t - 2])
        if 0 <= t - 3 < ng:
            put_back(t - 3, halves[t - 3])
    for c in sent:
        c.wait_send()


def write_kernel(*refs):
    n = (len(refs) - 1) // 2
    copies = [
        pltpu.make_async_copy(refs[i], refs[n + i], refs[2 * n].at[i]) for i in range(n)
    ]
    for c in copies:
        c.start()
    for c in copies:
        c.wait()


def shards(grad_parts, bucket_order, master, first_moment, second_moment, step_count, max_rms):
    _, rows, width = grad_parts.shape
    own_rows = master.shape[2]
    nr, ng = width // 2 // WR, width // WG
    entries = float(rows * width * lax.axis_size("x"))
    dma = pltpu.SemaphoreType.DMA
    anywhere = pl.BlockSpec(memory_space=pl.ANY)
    smem = pl.BlockSpec(memory_space=pltpu.SMEM)
    vmem = pl.BlockSpec(memory_space=pltpu.VMEM)
    state = pltpu.VMEM(master.shape, F32)
    results = pl.pallas_call(
        functools.partial(main_kernel, (rows, width, nr, ng, entries)),
        out_shape=(pltpu.VMEM((rows, width), BF16), state, state, state),
        in_specs=[smem] * 3 + [pl.BlockSpec(memory_space=pltpu.HBM)] * 4,
        out_specs=[vmem] * 4,
        scratch_shapes=[
            pltpu.VMEM((nr, rows, WR), BF16),
            pltpu.VMEM((nr, rows, WR), BF16),
            pltpu.VMEM((nr, N, N, 32, WR), BF16),
            pltpu.VMEM((nr, 2, 2, 32, WR), BF16),
            pltpu.VMEM((nr, 2, N, 32, WR), BF16),
            pltpu.VMEM((nr, 3, 32, WR), BF16),
            pltpu.VMEM((nr, 3, 32, WR), BF16),
            pltpu.VMEM((nr, 2, 16, WR), F32),
            pltpu.VMEM((own_rows, width), F32),
            pltpu.VMEM((N, N, 2, own_rows, width), BF16),
            pltpu.VMEM((rows, rows), BF16),
            pltpu.VMEM((rows, rows), BF16),
            pltpu.VMEM((3, own_rows, width), F32),
            pltpu.VMEM((2, own_rows, 128), F32),
            pltpu.VMEM((8, 128), F32),
            pltpu.VMEM((2 * N, 8, 128), F32),
            pltpu.VMEM((N * N, 8, 128), F32),
            dma((nr,)),
            dma((2, nr)),
            dma((2, nr, 2)),
            dma((2, nr, 4)),
            dma((2, nr, 3)),
            dma((2, nr)),
            dma((3,)),
            dma((2, 7)),
            dma((2, 15)),
            dma((2, ng, 3)),
            dma((2, ng, 2)),
            dma((2, ng, 2)),
            dma((2, ng)),
        ],
        compiler_params=pltpu.CompilerParams(
            collective_id=0, has_side_effects=True, vmem_limit_bytes=48 << 20
        ),
    )(bucket_order, step_count, max_rms, grad_parts, master, first_moment, second_moment)
    fresh, *moved = pl.pallas_call(
        write_kernel,
        out_shape=[jax.ShapeDtypeStruct(r.shape, r.dtype) for r in results],
        in_specs=[anywhere] * 4,
        out_specs=[pl.BlockSpec(memory_space=pltpu.HBM)] * 4,
        scratch_shapes=[dma((4,))],
        compiler_params=pltpu.CompilerParams(vmem_limit_bytes=1 << 20),
    )(*(pltpu.with_memory_space_constraint(r, pltpu.VMEM) for r in results))
    return (*moved, fresh)


def solution(mesh):
    dp = ("y", "z", "c")
    finer = Mesh(mesh.devices.reshape(N, N, 2, mesh.shape["expert"]), (*dp, "x"))
    state = P("x", dp, None, None)
    return jax.shard_map(
        shards,
        mesh=finer,
        in_specs=(P(dp, "x", None), P(), state, state, state, P("x", dp, None), P()),
        out_specs=(state, state, state, P("x", None)),
        check_vma=False,
    )
```

```python
import functools

import jax
import jax.numpy as jnp
from jax import lax
from jax.experimental import pallas as pl
from jax.experimental.pallas import tpu as pltpu
from jax.sharding import Mesh
from jax.sharding import PartitionSpec as P

MESH = pl.DeviceIdType.MESH
BF16, F32 = jnp.bfloat16, jnp.float32
N = 4
WR = 512
WG = 1024
TILE = 256
RS_LAG = (6, 6, 6)
AG_LAG = (6, 6, 1)


def away(axis, by, n=N):
    return lax.rem(lax.axis_index(axis) + by, n)


def main_kernel(
    sizes, order_in, steps_in, max_rms_in, grad, master, first, second,
    out, new_master, new_first, new_second,
    own, sib, sb, hop, fin, s2, r2, tot, gsum, slots, perm, perm_t, st, fix, sq, s1, s2nd, order, steps, max_rms,
    load_sem, pair_sem, hop_sem, fin_sem, r2_sem, tot_sem, st_sem, x_sem, yz_sem, p1_sem, p2_sem, fwd_sem, half_sem, small_sem, met_sem,
):
    rows, width, nr, ng, entries = sizes
    my, mz, mc, mx = (lax.axis_index(a) for a in "yzcx")
    half = width // 2
    coords = {"y": my, "z": mz}

    def axes(block):
        return ("y", "z") if block % 2 == 0 else ("z", "y")

    def remote(src, dst, sems, at, where):
        return pltpu.make_async_remote_copy(
            src_ref=src, dst_ref=dst, send_sem=sems.at[(0, *at)], recv_sem=sems.at[(1, *at)],
            device_id=where, device_id_type=MESH,
        )

    sent = []

    def start(copies):
        for c in copies:
            c.start()
        sent.extend(copies)
        return copies

    def arrived(copies):
        for c in copies:
            c.wait_recv()

    def load(k):
        cols = pl.ds(pl.multiple_of(mc * half + k * WR, WR), WR)
        return pltpu.make_async_copy(grad.at[0, :, cols], own.at[k], load_sem.at[k])

    loads = [load(k) for k in range(nr)]
    states = [
        pltpu.make_async_copy(a.at[0, 0], st.at[i], st_sem.at[i])
        for i, a in enumerate((master, first, second))
    ]
    small = [
        pltpu.make_async_copy(a, b, small_sem.at[i])
        for i, (a, b) in enumerate(((order_in, order), (steps_in, steps), (max_rms_in, max_rms)))
    ]
    for c in [*small, *loads, *states]:
        c.start()

    sibling = {"c": 1 - mc}
    group_x = [(i, j) for i in range(N) for j in range(2) if i or j]
    group_yz = [(i, j) for i in range(N) for j in range(N) if i or j]
    peers_x = [{"x": away("x", i), "c": away("c", j, 2)} for i, j in group_x]
    peers_yz = [{"y": away("y", i), "z": away("z", j)} for i, j in group_yz]
    def signal(sem, where):
        pl.semaphore_signal(sem, inc=1, device_id=where, device_id_type=MESH)

    beside_x = [{"x": away("x", 1)}, {"x": away("x", 3)}]
    nearest = [sibling, *({a: away(a, d)} for a in "yz" for d in (1, 3)), *beside_x]
    barrier = pltpu.get_barrier_semaphore()
    for peer in nearest:
        signal(barrier, peer)

    def fill(t, _):
        i = lax.broadcasted_iota(jnp.int32, (16, rows), 0)
        picked = jnp.zeros((16, rows), jnp.int32)
        for b in range(8):
            picked = jnp.where(i // 2 == b, order[t * 8 + b] * 2, picked)
        hit = lax.broadcasted_iota(jnp.int32, (16, rows), 1) == picked + i % 2
        perm[pl.ds(pl.multiple_of(t * 16, 16), 16), :] = jnp.where(hit, 1.0, 0.0).astype(BF16)
        return 0

    small[0].wait()
    lax.fori_loop(0, rows // 16, fill, 0)
    pl.semaphore_wait(barrier, len(nearest))

    def pair(k):
        cols = pl.ds(pl.multiple_of((1 - mc) * half + k * WR, WR), WR)
        return remote(grad.at[0, :, cols], sib.at[k], pair_sem, (k,), sibling)

    pairs = start([pair(k) for k in range(nr)])
    for peer in beside_x:
        signal(met_sem.at[0], peer)

    def pick_rows(k):
        loads[k].wait()
        arrived([pairs[k]])
        for t in range(WR // TILE):
            cols = pl.ds(t * TILE, TILE)
            both = own[k, :, cols].astype(F32) + sib[k, :, cols].astype(F32)
            moved = jnp.dot(perm[...], both.astype(BF16), preferred_element_type=F32)
            moved = moved.astype(BF16).reshape(N, N, 32, TILE)
            for i in range(N):
                for j in range(N):
                    at = (i, j) if k % 2 == 0 else (j, i)
                    sb[k, at[0], at[1], :, cols] = moved[i, j]

    def beside(axis):
        return coords[axis], away(axis, 1), away(axis, 2), away(axis, 3)

    lo, hi = pl.ds(0, 2), pl.ds(2, 2)

    def first_hops(k):
        a = axes(k)[0]
        _, up, far, down = beside(a)
        hops = [
            remote(sb.at[k, far, lo], hop.at[k, 0], hop_sem, (k, 0), {a: up}),
            remote(sb.at[k, far, hi], hop.at[k, 1], hop_sem, (k, 1), {a: down}),
        ]
        plain = [
            remote(sb.at[k, up, hi], fin.at[k, 0, hi], fin_sem, (k, 0), {a: up}),
            remote(sb.at[k, down, lo], fin.at[k, 1, lo], fin_sem, (k, 1), {a: down}),
        ]
        return start(hops), start(plain)

    def add_into(k, to, j0, slot):
        def body(i, _):
            j, r = i // 2, pl.ds(pl.multiple_of((i % 2) * 16, 16), 16)
            total = sb[k, to, j0 + j, r, :].astype(F32) + hop[k, slot, j, r, :].astype(F32)
            sb[k, to, j0 + j, r, :] = total.astype(BF16)
            return 0

        lax.fori_loop(0, 4, body, 0)

    def second_hops(k, hops):
        a = axes(k)[0]
        _, up, _, down = beside(a)
        arrived([hops[0]])
        add_into(k, up, 0, 0)
        one = remote(sb.at[k, up, lo], fin.at[k, 0, lo], fin_sem, (k, 2), {a: up})
        start([one])
        arrived([hops[1]])
        add_into(k, down, 2, 1)
        two = remote(sb.at[k, down, hi], fin.at[k, 1, hi], fin_sem, (k, 3), {a: down})
        start([two])
        return [one, two]

    def sum3(k, me, j, r):
        return sb[k, me, j, r, :].astype(F32) + fin[k, 0, j, r, :].astype(F32) + fin[k, 1, j, r, :].astype(F32)

    def across(k, waits):
        a, b = axes(k)
        me = coords[a]
        arrived(waits)
        copies = []
        for d in (2, 1, 3):
            j = away(b, d)

            def body(i, _, j=j, d=d):
                r = pl.ds(pl.multiple_of(i * 16, 16), 16)
                s2[k, d - 1, r, :] = sum3(k, me, j, r).astype(BF16)
                return 0

            lax.fori_loop(0, 2, body, 0)
            copies += start([remote(s2.at[k, d - 1], r2.at[k, d - 1], r2_sem, (k, d - 1), {b: j})])
        return copies

    def finish(k, waits):
        a, b = axes(k)
        me, mj = coords[a], coords[b]
        arrived(waits)
        cols = pl.ds(pl.multiple_of(mc * half + k * WR, WR), WR)
        for i in range(2):
            r = pl.ds(i * 16, 16)
            total = sum3(k, me, mj, r)
            for d in range(3):
                total = total + r2[k, d, r, :].astype(F32)
            tot[k, i] = total
            square = total * total
            folded = square[:, :128]
            for t in range(1, WR // 128):
                folded = folded + square[:, t * 128 : (t + 1) * 128]
            sq[...] += folded[:8] + folded[8:]
        gsum[:, cols] = tot[k, mc]
        return start([remote(tot.at[k, 1 - mc], gsum.at[:, cols], tot_sem, (k,), sibling)])

    sq[...] = jnp.zeros_like(sq)
    hops, plain, second_half, sums, shared = {}, {}, {}, {}, []
    for t in range(nr + sum(RS_LAG)):
        if t < nr:
            pick_rows(t)
            hops[t], plain[t] = first_hops(t)
        k = t - RS_LAG[0]
        if 0 <= k < nr:
            second_half[k] = second_hops(k, hops[k])
        k -= RS_LAG[1]
        if k == 0:
            pl.semaphore_wait(met_sem.at[0], 2)
            for peer in beside_x:
                signal(met_sem.at[1], peer)
        if 0 <= k < nr:
            sums[k] = across(k, plain[k] + second_half[k])
        k -= RS_LAG[2]
        if 0 <= k < nr:
            shared += finish(k, sums[k])

    mine_x, mine_yz = mx * 2 + mc, my * N + mz
    s1[mine_x] = sq[...]
    pl.semaphore_wait(met_sem.at[1], 2)
    across_x = start([
        remote(sq, s1.at[mine_x], x_sem, (n,), peer) for n, peer in enumerate(peers_x)
    ])

    def flip(t, _):
        r = pl.ds(pl.multiple_of(t * 128, 128), 128)
        i = lax.broadcasted_iota(jnp.int32, (128, rows), 0) + t * 128
        eye = jnp.where(i == lax.broadcasted_iota(jnp.int32, (128, rows), 1), 1.0, 0.0).astype(BF16)
        perm_t[r, :] = lax.dot_general(
            eye, perm[...], (((1,), (1,)), ((), ())), preferred_element_type=F32
        ).astype(BF16)
        return 0

    lax.fori_loop(0, rows // 128, flip, 0)
    small[1].wait()
    small[2].wait()
    lane_row = lax.broadcasted_iota(jnp.int32, (16, 128), 0)
    count = jnp.zeros((16, 128), jnp.int32)
    for i in range(16):
        count = jnp.where(lane_row == i, steps[0, 0, i], count)
    count = count.astype(F32)
    fix[0] = 1.0 - jnp.power(jnp.full((16, 128), 0.9, F32), count)
    fix[1] = 1.0 - jnp.power(jnp.full((16, 128), 0.95, F32), count)
    for c in states:
        c.wait()

    arrived(across_x)
    part = s1[0]
    for i in range(1, 2 * N):
        part = part + s1[i]
    s2nd[mine_yz] = part
    mine = s2nd.at[mine_yz]
    across_yz = start([remote(mine, mine, yz_sem, (n,), peer) for n, peer in enumerate(peers_yz)])
    arrived(shared)
    arrived(across_yz)
    part = s2nd[0]
    for i in range(1, N * N):
        part = part + s2nd[i]
    square_sum = jnp.sum(jnp.sum(part, axis=1, keepdims=True), axis=0, keepdims=True)
    clip = jnp.minimum(1.0, max_rms[0] / jnp.sqrt(square_sum / entries + 1e-06))

    def update(k):
        def body(t, _):
            cols = pl.ds(pl.multiple_of(k * WG + t * 128, 128), 128)
            clipped = clip * gsum[:, cols]
            moment = 0.9 * st[1, :, cols] + 0.1 * clipped
            variance = 0.95 * st[2, :, cols] + 0.05 * clipped * clipped
            ratio = moment / fix[0] / (jnp.sqrt(variance / fix[1]) + 1e-08)
            old = st[0, :, cols]
            fresh = old - 0.1 * (ratio + 0.1 * old)
            new_master[0, 0, :, cols] = fresh
            new_first[0, 0, :, cols] = moment
            new_second[0, 0, :, cols] = variance
            slots[my, mz, mc, :, cols] = fresh.astype(BF16)
            return 0

        lax.fori_loop(0, WG // 128, body, 0)
        cols = pl.ds(k * WG, WG)
        a = axes(k)[0]
        mine = slots.at[my, mz, mc, :, cols]
        return start([remote(mine, mine, p1_sem, (k, d - 1), {a: away(a, d)}) for d in (2, 1, 3)])

    def row(k, at, part):
        cols = pl.ds(k * WG, WG)
        if k % 2 == 0:
            return slots.at[part, at, mc, :, cols]
        return slots.at[at, part, mc, :, cols]

    def spread(k, waits):
        arrived(waits)
        b = axes(k)[1]
        me, up, _, down = beside(b)
        mine = row(k, me, pl.ds(0, N))
        return start([
            remote(mine, mine, p2_sem, (k, 0), {b: up}),
            remote(mine, mine, p2_sem, (k, 1), {b: down}),
        ])

    def forward(k, waits):
        b = axes(k)[1]
        _, up, _, down = beside(b)
        arrived(waits[:1])
        one, two = row(k, down, lo), row(k, up, hi)
        copies = start([remote(one, one, fwd_sem, (k, 0), {b: up})])
        arrived(waits[1:])
        return copies + start([remote(two, two, fwd_sem, (k, 1), {b: down})])

    def to_sibling(k, waits):
        arrived(waits)
        block = slots.at[:, :, mc, :, pl.ds(k * WG, WG)]
        return start([remote(block, block, half_sem, (k,), sibling)])

    def put_back(k, waits):
        arrived(waits)
        for t in range(WG // TILE):
            cols = pl.ds(k * WG + t * TILE, TILE)
            block = slots[:, :, :, :, cols].reshape(rows, TILE)
            out[:, cols] = jnp.dot(perm_t[...], block, preferred_element_type=F32).astype(BF16)

    ups = [update(k) for k in range(ng)]
    across_b, forwards, halves = {}, {}, {}
    for t in range(ng + sum(AG_LAG)):
        if t < ng:
            across_b[t] = spread(t, ups[t])
        k = t - AG_LAG[0]
        if 0 <= k < ng:
            forwards[k] = forward(k, across_b[k])
        k -= AG_LAG[1]
        if 0 <= k < ng:
            halves[k] = to_sibling(k, forwards[k])
        k -= AG_LAG[2]
        if 0 <= k < ng:
            put_back(k, halves[k])
    for c in sent:
        c.wait_send()


def write_kernel(*refs):
    n = (len(refs) - 1) // 2
    sem = refs[2 * n]
    copies = [
        pltpu.make_async_copy(refs[0].at[pl.ds(i * 64, 64)], refs[n].at[pl.ds(i * 64, 64)], sem.at[i])
        for i in range(8)
    ]
    copies += [
        pltpu.make_async_copy(refs[i], refs[n + i], sem.at[7 + i]) for i in range(1, n)
    ]
    for c in copies:
        c.start()
    for c in copies:
        c.wait()


def shards(grad_parts, bucket_order, master, first_moment, second_moment, step_count, max_rms):
    _, rows, width = grad_parts.shape
    own_rows = master.shape[2]
    nr, ng = width // 2 // WR, width // WG
    entries = float(rows * width * lax.axis_size("x"))
    dma = pltpu.SemaphoreType.DMA
    anywhere = pl.BlockSpec(memory_space=pl.ANY)
    vmem = pl.BlockSpec(memory_space=pltpu.VMEM)
    state = pltpu.VMEM(master.shape, F32)
    results = pl.pallas_call(
        functools.partial(main_kernel, (rows, width, nr, ng, entries)),
        out_shape=(pltpu.VMEM((rows, width), BF16), state, state, state),
        in_specs=[pl.BlockSpec(memory_space=pltpu.HBM)] * 7,
        out_specs=[vmem] * 4,
        scratch_shapes=[
            pltpu.VMEM((nr, rows, WR), BF16),
            pltpu.VMEM((nr, rows, WR), BF16),
            pltpu.VMEM((nr, N, N, 32, WR), BF16),
            pltpu.VMEM((nr, 2, 2, 32, WR), BF16),
            pltpu.VMEM((nr, 2, N, 32, WR), BF16),
            pltpu.VMEM((nr, 3, 32, WR), BF16),
            pltpu.VMEM((nr, 3, 32, WR), BF16),
            pltpu.VMEM((nr, 2, 16, WR), F32),
            pltpu.VMEM((own_rows, width), F32),
            pltpu.VMEM((N, N, 2, own_rows, width), BF16),
            pltpu.VMEM((rows, rows), BF16),
            pltpu.VMEM((rows, rows), BF16),
            pltpu.VMEM((3, own_rows, width), F32),
            pltpu.VMEM((2, own_rows, 128), F32),
            pltpu.VMEM((8, 128), F32),
            pltpu.VMEM((2 * N, 8, 128), F32),
            pltpu.VMEM((N * N, 8, 128), F32),
            pltpu.SMEM(bucket_order.shape, jnp.int32),
            pltpu.SMEM(step_count.shape, jnp.int32),
            pltpu.SMEM(max_rms.shape, F32),
            dma((nr,)),
            dma((2, nr)),
            dma((2, nr, 2)),
            dma((2, nr, 4)),
            dma((2, nr, 3)),
            dma((2, nr)),
            dma((3,)),
            dma((2, 7)),
            dma((2, 15)),
            dma((2, ng, 3)),
            dma((2, ng, 2)),
            dma((2, ng, 2)),
            dma((2, ng)),
            dma((3,)),
            pltpu.SemaphoreType.REGULAR((2,)),
        ],
        compiler_params=pltpu.CompilerParams(
            collective_id=0, has_side_effects=True, vmem_limit_bytes=48 << 20
        ),
    )(bucket_order, step_count, max_rms, grad_parts, master, first_moment, second_moment)
    fresh, *moved = pl.pallas_call(
        write_kernel,
        out_shape=[jax.ShapeDtypeStruct(r.shape, r.dtype) for r in results],
        in_specs=[anywhere] * 4,
        out_specs=[pl.BlockSpec(memory_space=pltpu.HBM)] * 4,
        scratch_shapes=[dma((11,))],
        compiler_params=pltpu.CompilerParams(vmem_limit_bytes=1 << 20),
    )(*(pltpu.with_memory_space_constraint(r, pltpu.VMEM) for r in results))
    return (*moved, fresh)


def solution(mesh):
    dp = ("y", "z", "c")
    finer = Mesh(mesh.devices.reshape(N, N, 2, mesh.shape["expert"]), (*dp, "x"))
    state = P("x", dp, None, None)
    return jax.shard_map(
        shards,
        mesh=finer,
        in_specs=(P(dp, "x", None), P(), state, state, state, P("x", dp, None), P()),
        out_specs=(state, state, state, P("x", None)),
        check_vma=False,
    )
```

```python
import functools

import jax
import jax.numpy as jnp
from jax import lax
from jax.experimental import pallas as pl
from jax.experimental.pallas import tpu as pltpu
from jax.sharding import Mesh
from jax.sharding import PartitionSpec as P

MESH = pl.DeviceIdType.MESH
BF16, F32 = jnp.bfloat16, jnp.float32
N = 4
WR = 512
WG = 512
TILE = 256
WU = 512
RS_LAG = (6, 6, 6)
AG_LAG = (6, 6, 2)


def main_kernel(
    sizes, order_in, steps_in, max_rms_in, grad, master, first, second,
    out, new_master, new_first, new_second,
    own, sib, sb, hop, fin, s2, r2, tot, gsum, slots, perm, perm_t, st, fix, sq, s1, s2nd, order, steps, max_rms,
    load_sem, pair_sem, hop_sem, fin_sem, r2_sem, tot_sem, st_sem, x_sem, yz_sem, p1_sem, p2_sem, fwd_sem, half_sem, small_sem, met_sem,
):
    rows, width, nr, ng, entries = sizes
    my, mz, mc, mx = (lax.axis_index(a) for a in "yzcx")
    half = width // 2
    coords = {"y": my, "z": mz}
    ring = {a: [lax.rem(lax.axis_index(a) + d, N) for d in range(N)] for a in "yzx"}

    def device(y=my, z=mz, c=mc, x=mx):
        return y, z, c, x

    at = {a: [device(**{a: ring[a][d]}) for d in range(N)] for a in "yzx"}
    sibling = device(c=1 - mc)

    def axes(block):
        return ("y", "z") if block % 2 == 0 else ("z", "y")

    def send(src, dst, sems, n, where):
        pltpu.make_async_remote_copy(
            src_ref=src, dst_ref=dst, send_sem=sems.at[0], recv_sem=sems.at[1 + n],
            device_id=where, device_id_type=MESH,
        ).start()

    def wait(ref, sem):
        pltpu.make_async_remote_copy(
            src_ref=ref, dst_ref=ref, send_sem=sem, recv_sem=sem,
            device_id=sibling, device_id_type=MESH,
        ).wait_recv()

    def load(k):
        cols = pl.ds(pl.multiple_of(mc * half + k * WR, WR), WR)
        return pltpu.make_async_copy(grad.at[0, :, cols], own.at[k], load_sem.at[k])

    loads = [load(k) for k in range(nr)]
    states = [
        pltpu.make_async_copy(a.at[0, 0], st.at[i], st_sem.at[i])
        for i, a in enumerate((master, first, second))
    ]
    small = [
        pltpu.make_async_copy(a, b, small_sem.at[i])
        for i, (a, b) in enumerate(((order_in, order), (steps_in, steps), (max_rms_in, max_rms)))
    ]
    for c in [*small, *loads, *states]:
        c.start()

    peers_x = [device(x=ring["x"][i], c=c) for i in range(N) for c in (mc, 1 - mc)][1:]
    peers_yz = [device(y=ring["y"][i], z=ring["z"][j]) for i in range(N) for j in range(N)][1:]

    def signal(sem, where):
        pl.semaphore_signal(sem, inc=1, device_id=where, device_id_type=MESH)

    beside_x = [at["x"][1], at["x"][3]]
    nearest = [sibling, *(at[a][d] for a in "yz" for d in (1, 3)), *beside_x]
    barrier = pltpu.get_barrier_semaphore()
    for peer in nearest:
        signal(barrier, peer)

    def fill(t, _):
        i = lax.broadcasted_iota(jnp.int32, (16, rows), 0)
        picked = jnp.zeros((16, rows), jnp.int32)
        for b in range(8):
            picked = jnp.where(i // 2 == b, order[t * 8 + b] * 2, picked)
        hit = lax.broadcasted_iota(jnp.int32, (16, rows), 1) == picked + i % 2
        perm[pl.ds(pl.multiple_of(t * 16, 16), 16), :] = jnp.where(hit, 1.0, 0.0).astype(BF16)
        return 0

    small[0].wait()
    lax.fori_loop(0, rows // 16, fill, 0)
    pl.semaphore_wait(barrier, len(nearest))

    for k in range(nr):
        cols = pl.ds(pl.multiple_of((1 - mc) * half + k * WR, WR), WR)
        send(grad.at[0, :, cols], sib.at[k], pair_sem, k, sibling)
    for peer in beside_x:
        signal(met_sem.at[0], peer)

    def pick_rows(k):
        loads[k].wait()
        wait(sib.at[k], pair_sem.at[1 + k])
        for t in range(WR // TILE):
            cols = pl.ds(t * TILE, TILE)
            both = own[k, :, cols].astype(F32) + sib[k, :, cols].astype(F32)
            moved = jnp.dot(perm[...], both.astype(BF16), preferred_element_type=F32)
            moved = moved.astype(BF16).reshape(N, N, 32, TILE)
            for i in range(N):
                for j in range(N):
                    at = (i, j) if k % 2 == 0 else (j, i)
                    sb[k, at[0], at[1], :, cols] = moved[i, j]

    lo, hi = pl.ds(0, 2), pl.ds(2, 2)

    def first_hops(k):
        a = axes(k)[0]
        _, up, far, down = ring[a]
        send(sb.at[k, far, lo], hop.at[k, 0], hop_sem, k, at[a][1])
        send(sb.at[k, far, hi], hop.at[k, 1], hop_sem, k, at[a][3])
        send(sb.at[k, up, hi], fin.at[k, 0, hi], fin_sem, k, at[a][1])
        send(sb.at[k, down, lo], fin.at[k, 1, lo], fin_sem, k, at[a][3])

    def second_hops(k):
        a = axes(k)[0]
        _, up, _, down = ring[a]
        wait(hop.at[k], hop_sem.at[1 + k])
        for slot, to, part in ((0, up, lo), (1, down, hi)):

            def body(i, _, slot=slot, to=to):
                r = pl.ds(pl.multiple_of(i * 16, 16), 16)
                for j in range(2):
                    mine = sb[k, to, 2 * slot + j, r, :].astype(F32)
                    sb[k, to, 2 * slot + j, r, :] = (mine + hop[k, slot, j, r, :].astype(F32)).astype(BF16)
                return 0

            lax.fori_loop(0, 2, body, 0)
            send(sb.at[k, to, part], fin.at[k, slot, part], fin_sem, k, at[a][1 + 2 * slot])

    def sum3(k, me, j, r):
        return sb[k, me, j, r, :].astype(F32) + fin[k, 0, j, r, :].astype(F32) + fin[k, 1, j, r, :].astype(F32)

    def across(k):
        a, b = axes(k)
        me = coords[a]
        wait(fin.at[k], fin_sem.at[1 + k])
        for d in (2, 1, 3):
            j = ring[b][d]

            def body(i, _, j=j, d=d):
                r = pl.ds(pl.multiple_of(i * 16, 16), 16)
                s2[k, d - 1, r, :] = sum3(k, me, j, r).astype(BF16)
                return 0

            lax.fori_loop(0, 2, body, 0)
            send(s2.at[k, d - 1], r2.at[k, d - 1], r2_sem, k, at[b][d])

    def finish(k):
        a, b = axes(k)
        me, mj = coords[a], coords[b]
        wait(r2.at[k], r2_sem.at[1 + k])
        cols = pl.ds(pl.multiple_of(mc * half + k * WR, WR), WR)
        for i in range(2):
            r = pl.ds(i * 16, 16)
            total = sum3(k, me, mj, r)
            for d in range(3):
                total = total + r2[k, d, r, :].astype(F32)
            tot[k, i] = total
            square = total * total
            folded = square[:, :128]
            for t in range(1, WR // 128):
                folded = folded + square[:, t * 128 : (t + 1) * 128]
            sq[...] += folded[:8] + folded[8:]
        gsum[:, cols] = tot[k, mc]
        send(tot.at[k, 1 - mc], gsum.at[:, cols], tot_sem, 0, sibling)

    sq[...] = jnp.zeros_like(sq)
    for t in range(nr + sum(RS_LAG)):
        if t < nr:
            pick_rows(t)
            first_hops(t)
        k = t - RS_LAG[0]
        if 0 <= k < nr:
            second_hops(k)
        k -= RS_LAG[1]
        if k == 0:
            pl.semaphore_wait(met_sem.at[0], 2)
            for peer in beside_x:
                signal(met_sem.at[1], peer)
        if 0 <= k < nr:
            across(k)
        k -= RS_LAG[2]
        if 0 <= k < nr:
            finish(k)

    mine_x, mine_yz = mx * 2 + mc, my * N + mz
    s1[mine_x] = sq[...]
    pl.semaphore_wait(met_sem.at[1], 2)
    for peer in peers_x:
        send(sq, s1.at[mine_x], x_sem, 0, peer)

    def flip(t, _):
        r = pl.ds(pl.multiple_of(t * 128, 128), 128)
        i = lax.broadcasted_iota(jnp.int32, (128, rows), 0) + t * 128
        eye = jnp.where(i == lax.broadcasted_iota(jnp.int32, (128, rows), 1), 1.0, 0.0).astype(BF16)
        perm_t[r, :] = lax.dot_general(
            eye, perm[...], (((1,), (1,)), ((), ())), preferred_element_type=F32
        ).astype(BF16)
        return 0

    lax.fori_loop(0, rows // 128, flip, 0)
    small[1].wait()
    small[2].wait()
    lane_row = lax.broadcasted_iota(jnp.int32, (16, WU), 0)
    count = jnp.zeros((16, WU), jnp.int32)
    for i in range(16):
        count = jnp.where(lane_row == i, steps[0, 0, i], count)
    count = count.astype(F32)
    fix[0] = 1.0 - jnp.power(jnp.full((16, WU), 0.9, F32), count)
    fix[1] = 1.0 - jnp.power(jnp.full((16, WU), 0.95, F32), count)
    for c in states:
        c.wait()

    for ref, sems in ((sib, pair_sem), (hop, hop_sem), (fin, fin_sem), (r2, r2_sem)):
        wait(ref, sems.at[0])

    few = s1.at[pl.ds(0, len(peers_x))]
    many = s2nd.at[pl.ds(0, len(peers_yz))]
    wait(few, x_sem.at[1])
    part = s1[0]
    for i in range(1, 2 * N):
        part = part + s1[i]
    s2nd[mine_yz] = part
    mine = s2nd.at[mine_yz]
    for peer in peers_yz:
        send(mine, mine, yz_sem, 0, peer)
    given = gsum.at[:, pl.ds(0, half)]
    wait(few, x_sem.at[0])
    wait(given, tot_sem.at[0])
    wait(given, tot_sem.at[1])
    wait(many, yz_sem.at[1])
    part = s2nd[0]
    for i in range(1, N * N):
        part = part + s2nd[i]
    square_sum = jnp.sum(jnp.sum(part, axis=1, keepdims=True), axis=0, keepdims=True)
    clip = jnp.minimum(1.0, max_rms[0] / jnp.sqrt(square_sum / entries + 1e-06))

    def update(k):
        def body(t, _):
            cols = pl.ds(pl.multiple_of(k * WG + t * WU, WU), WU)
            clipped = clip * gsum[:, cols]
            moment = 0.9 * st[1, :, cols] + 0.1 * clipped
            variance = 0.95 * st[2, :, cols] + 0.05 * clipped * clipped
            ratio = moment / fix[0] / (jnp.sqrt(variance / fix[1]) + 1e-08)
            old = st[0, :, cols]
            fresh = old - 0.1 * (ratio + 0.1 * old)
            new_master[0, 0, :, cols] = fresh
            new_first[0, 0, :, cols] = moment
            new_second[0, 0, :, cols] = variance
            slots[my, mz, mc, :, cols] = fresh.astype(BF16)
            return 0

        lax.fori_loop(0, WG // WU, body, 0)
        cols = pl.ds(k * WG, WG)
        a = axes(k)[0]
        mine = slots.at[my, mz, mc, :, cols]
        for d in (2, 1, 3):
            send(mine, mine, p1_sem, k, at[a][d])

    def row(k, at, part):
        cols = pl.ds(k * WG, WG)
        if k % 2 == 0:
            return slots.at[part, at, mc, :, cols]
        return slots.at[at, part, mc, :, cols]

    def spread(k):
        b = axes(k)[1]
        wait(slots.at[0, pl.ds(0, 3), 0, :, pl.ds(k * WG, WG)], p1_sem.at[1 + k])
        mine = row(k, coords[b], pl.ds(0, N))
        for d in (1, 3):
            send(mine, mine, p2_sem, k, at[b][d])

    def forward(k):
        b = axes(k)[1]
        wait(slots.at[pl.ds(0, 2), :, 0, :, pl.ds(k * WG, WG)], p2_sem.at[1 + k])
        for d, part in ((1, lo), (3, hi)):
            block = row(k, ring[b][4 - d], part)
            send(block, block, fwd_sem, k, at[b][d])

    def to_sibling(k):
        wait(slots.at[0, :, 0, :, pl.ds(k * WG, WG)], fwd_sem.at[1 + k])
        block = slots.at[:, :, mc, :, pl.ds(k * WG, WG)]
        send(block, block, half_sem, k, sibling)

    def put_back(k):
        wait(slots.at[:, :, 0, :, pl.ds(k * WG, WG)], half_sem.at[1 + k])
        for t in range(WG // TILE):
            cols = pl.ds(k * WG + t * TILE, TILE)
            block = slots[:, :, :, :, cols].reshape(rows, TILE)
            out[:, cols] = jnp.dot(perm_t[...], block, preferred_element_type=F32).astype(BF16)

    for k in range(ng):
        update(k)
    for t in range(ng + sum(AG_LAG)):
        if t < ng:
            spread(t)
        k = t - AG_LAG[0]
        if 0 <= k < ng:
            forward(k)
        k -= AG_LAG[1]
        if 0 <= k < ng:
            to_sibling(k)
        k -= AG_LAG[2]
        if 0 <= k < ng:
            put_back(k)
    wait(many, yz_sem.at[0])
    wait(slots.at[0, pl.ds(0, 3), 0], p1_sem.at[0])
    wait(slots.at[pl.ds(0, 2), :, 0], p2_sem.at[0])
    wait(slots.at[0, :, 0], fwd_sem.at[0])
    wait(slots.at[:, :, 0], half_sem.at[0])


def write_kernel(*refs):
    n = (len(refs) - 1) // 2
    sem = refs[2 * n]
    copies = [
        pltpu.make_async_copy(refs[0].at[pl.ds(i * 64, 64)], refs[n].at[pl.ds(i * 64, 64)], sem.at[i])
        for i in range(8)
    ]
    copies += [
        pltpu.make_async_copy(refs[i], refs[n + i], sem.at[7 + i]) for i in range(1, n)
    ]
    for c in copies:
        c.start()
    for c in copies:
        c.wait()


def shards(grad_parts, bucket_order, master, first_moment, second_moment, step_count, max_rms):
    _, rows, width = grad_parts.shape
    own_rows = master.shape[2]
    nr, ng = width // 2 // WR, width // WG
    entries = float(rows * width * lax.axis_size("x"))
    dma = pltpu.SemaphoreType.DMA
    anywhere = pl.BlockSpec(memory_space=pl.ANY)
    vmem = pl.BlockSpec(memory_space=pltpu.VMEM)
    state = pltpu.VMEM(master.shape, F32)
    results = pl.pallas_call(
        functools.partial(main_kernel, (rows, width, nr, ng, entries)),
        out_shape=(pltpu.VMEM((rows, width), BF16), state, state, state),
        in_specs=[pl.BlockSpec(memory_space=pltpu.HBM)] * 7,
        out_specs=[vmem] * 4,
        scratch_shapes=[
            pltpu.VMEM((nr, rows, WR), BF16),
            pltpu.VMEM((nr, rows, WR), BF16),
            pltpu.VMEM((nr, N, N, 32, WR), BF16),
            pltpu.VMEM((nr, 2, 2, 32, WR), BF16),
            pltpu.VMEM((nr, 2, N, 32, WR), BF16),
            pltpu.VMEM((nr, 3, 32, WR), BF16),
            pltpu.VMEM((nr, 3, 32, WR), BF16),
            pltpu.VMEM((nr, 2, 16, WR), F32),
            pltpu.VMEM((own_rows, width), F32),
            pltpu.VMEM((N, N, 2, own_rows, width), BF16),
            pltpu.VMEM((rows, rows), BF16),
            pltpu.VMEM((rows, rows), BF16),
            pltpu.VMEM((3, own_rows, width), F32),
            pltpu.VMEM((2, own_rows, WU), F32),
            pltpu.VMEM((8, 128), F32),
            pltpu.VMEM((2 * N, 8, 128), F32),
            pltpu.VMEM((N * N, 8, 128), F32),
            pltpu.SMEM(bucket_order.shape, jnp.int32),
            pltpu.SMEM(step_count.shape, jnp.int32),
            pltpu.SMEM(max_rms.shape, F32),
            dma((nr,)),
            *[dma((1 + nr,))] * 4,
            dma((2,)),
            dma((3,)),
            *[dma((2,))] * 2,
            *[dma((1 + ng,))] * 4,
            dma((3,)),
            pltpu.SemaphoreType.REGULAR((2,)),
        ],
        compiler_params=pltpu.CompilerParams(
            collective_id=0, has_side_effects=True, vmem_limit_bytes=48 << 20
        ),
    )(bucket_order, step_count, max_rms, grad_parts, master, first_moment, second_moment)
    fresh, *moved = pl.pallas_call(
        write_kernel,
        out_shape=[jax.ShapeDtypeStruct(r.shape, r.dtype) for r in results],
        in_specs=[anywhere] * 4,
        out_specs=[pl.BlockSpec(memory_space=pltpu.HBM)] * 4,
        scratch_shapes=[dma((11,))],
        compiler_params=pltpu.CompilerParams(vmem_limit_bytes=1 << 20),
    )(*(pltpu.with_memory_space_constraint(r, pltpu.VMEM) for r in results))
    return (*moved, fresh)


def solution(mesh):
    dp = ("y", "z", "c")
    finer = Mesh(mesh.devices.reshape(N, N, 2, mesh.shape["expert"]), (*dp, "x"))
    state = P("x", dp, None, None)
    return jax.shard_map(
        shards,
        mesh=finer,
        in_specs=(P(dp, "x", None), P(), state, state, state, P("x", dp, None), P()),
        out_specs=(state, state, state, P("x", None)),
        check_vma=False,
    )
```

```python
import functools

import jax
import jax.numpy as jnp
from jax import lax
from jax.experimental import pallas as pl
from jax.experimental.pallas import tpu as pltpu
from jax.sharding import Mesh
from jax.sharding import PartitionSpec as P

MESH = pl.DeviceIdType.MESH
BF16, F32 = jnp.bfloat16, jnp.float32
N = 4
WR = 512
WG = 512
TILE = 256
WU = 512
RS_LAG = (6, 6, 6)
AG_LAG = (6, 6, 2)
LATE = 6


def restore(slots, perm_t, out, start, to):
    rows = perm_t.shape[0]
    for t in range(WG // TILE):
        block = slots[:, :, :, :, pl.ds(start + t * TILE, TILE)].reshape(rows, TILE)
        moved = jnp.dot(perm_t[...], block, preferred_element_type=F32)
        out[:, pl.ds(to + t * TILE, TILE)] = moved.astype(BF16)


def main_kernel(
    sizes, order_in, steps_in, max_rms_in, grad, master, first, second,
    out, new_master, new_first, new_second, slots, perm_t,
    own, sib, sb, hop, fin, s2, r2, tot, gsum, perm, st, fix, sq, s1, s2nd, order, steps, max_rms,
    load_sem, pair_sem, hop_sem, fin_sem, r2_sem, tot_sem, st_sem, x_sem, yz_sem, p1_sem, p2_sem, fwd_sem, half_sem, small_sem, met_sem,
):
    rows, width, nr, ng, entries = sizes
    my, mz, mc, mx = (lax.axis_index(a) for a in "yzcx")
    half = width // 2
    coords = {"y": my, "z": mz}
    ring = {a: [lax.rem(lax.axis_index(a) + d, N) for d in range(N)] for a in "yzx"}

    def device(y=my, z=mz, c=mc, x=mx):
        return y, z, c, x

    at = {a: [device(**{a: ring[a][d]}) for d in range(N)] for a in "yzx"}
    sibling = device(c=1 - mc)

    def axes(block):
        return ("y", "z") if block % 2 == 0 else ("z", "y")

    def send(src, dst, sems, n, where):
        pltpu.make_async_remote_copy(
            src_ref=src, dst_ref=dst, send_sem=sems.at[0], recv_sem=sems.at[1 + n],
            device_id=where, device_id_type=MESH,
        ).start()

    def wait(ref, sem):
        pltpu.make_async_remote_copy(
            src_ref=ref, dst_ref=ref, send_sem=sem, recv_sem=sem,
            device_id=sibling, device_id_type=MESH,
        ).wait_recv()

    def load(k):
        cols = pl.ds(pl.multiple_of(mc * half + k * WR, WR), WR)
        return pltpu.make_async_copy(grad.at[0, :, cols], own.at[k], load_sem.at[k])

    loads = [load(k) for k in range(nr)]
    states = [
        pltpu.make_async_copy(a.at[0, 0], st.at[i], st_sem.at[i])
        for i, a in enumerate((master, first, second))
    ]
    small = [
        pltpu.make_async_copy(a, b, small_sem.at[i])
        for i, (a, b) in enumerate(((order_in, order), (steps_in, steps), (max_rms_in, max_rms)))
    ]
    for c in [*small, *loads, *states]:
        c.start()

    peers_x = [device(x=ring["x"][i], c=c) for i in range(N) for c in (mc, 1 - mc)][1:]
    peers_yz = [device(y=ring["y"][i], z=ring["z"][j]) for i in range(N) for j in range(N)][1:]

    def signal(sem, where):
        pl.semaphore_signal(sem, inc=1, device_id=where, device_id_type=MESH)

    beside_x = [at["x"][1], at["x"][3]]
    nearest = [sibling, *(at[a][d] for a in "yz" for d in (1, 3)), *beside_x]
    barrier = pltpu.get_barrier_semaphore()
    for peer in nearest:
        signal(barrier, peer)

    def fill(t, _):
        i = lax.broadcasted_iota(jnp.int32, (16, rows), 0)
        picked = jnp.zeros((16, rows), jnp.int32)
        for b in range(8):
            picked = jnp.where(i // 2 == b, order[t * 8 + b] * 2, picked)
        hit = lax.broadcasted_iota(jnp.int32, (16, rows), 1) == picked + i % 2
        perm[pl.ds(pl.multiple_of(t * 16, 16), 16), :] = jnp.where(hit, 1.0, 0.0).astype(BF16)
        return 0

    small[0].wait()
    lax.fori_loop(0, rows // 16, fill, 0)
    pl.semaphore_wait(barrier, len(nearest))

    for k in range(nr):
        cols = pl.ds(pl.multiple_of((1 - mc) * half + k * WR, WR), WR)
        send(grad.at[0, :, cols], sib.at[k], pair_sem, k, sibling)
    for peer in beside_x:
        signal(met_sem.at[0], peer)

    def pick_rows(k):
        loads[k].wait()
        wait(sib.at[k], pair_sem.at[1 + k])
        for t in range(WR // TILE):
            cols = pl.ds(t * TILE, TILE)
            both = own[k, :, cols].astype(F32) + sib[k, :, cols].astype(F32)
            moved = jnp.dot(perm[...], both.astype(BF16), preferred_element_type=F32)
            moved = moved.astype(BF16).reshape(N, N, 32, TILE)
            for i in range(N):
                for j in range(N):
                    at = (i, j) if k % 2 == 0 else (j, i)
                    sb[k, at[0], at[1], :, cols] = moved[i, j]

    lo, hi = pl.ds(0, 2), pl.ds(2, 2)

    def first_hops(k):
        a = axes(k)[0]
        _, up, far, down = ring[a]
        send(sb.at[k, far, lo], hop.at[k, 0], hop_sem, k, at[a][1])
        send(sb.at[k, far, hi], hop.at[k, 1], hop_sem, k, at[a][3])
        send(sb.at[k, up, hi], fin.at[k, 0, hi], fin_sem, k, at[a][1])
        send(sb.at[k, down, lo], fin.at[k, 1, lo], fin_sem, k, at[a][3])

    def second_hops(k):
        a = axes(k)[0]
        _, up, _, down = ring[a]
        wait(hop.at[k], hop_sem.at[1 + k])
        for slot, to, part in ((0, up, lo), (1, down, hi)):

            def body(i, _, slot=slot, to=to):
                r = pl.ds(pl.multiple_of(i * 16, 16), 16)
                for j in range(2):
                    mine = sb[k, to, 2 * slot + j, r, :].astype(F32)
                    sb[k, to, 2 * slot + j, r, :] = (mine + hop[k, slot, j, r, :].astype(F32)).astype(BF16)
                return 0

            lax.fori_loop(0, 2, body, 0)
            send(sb.at[k, to, part], fin.at[k, slot, part], fin_sem, k, at[a][1 + 2 * slot])

    def sum3(k, me, j, r):
        return sb[k, me, j, r, :].astype(F32) + fin[k, 0, j, r, :].astype(F32) + fin[k, 1, j, r, :].astype(F32)

    def across(k):
        a, b = axes(k)
        me = coords[a]
        wait(fin.at[k], fin_sem.at[1 + k])
        for d in (2, 1, 3):
            j = ring[b][d]

            def body(i, _, j=j, d=d):
                r = pl.ds(pl.multiple_of(i * 16, 16), 16)
                s2[k, d - 1, r, :] = sum3(k, me, j, r).astype(BF16)
                return 0

            lax.fori_loop(0, 2, body, 0)
            send(s2.at[k, d - 1], r2.at[k, d - 1], r2_sem, k, at[b][d])

    def finish(k):
        a, b = axes(k)
        me, mj = coords[a], coords[b]
        wait(r2.at[k], r2_sem.at[1 + k])
        cols = pl.ds(pl.multiple_of(mc * half + k * WR, WR), WR)
        for i in range(2):
            r = pl.ds(i * 16, 16)
            total = sum3(k, me, mj, r)
            for d in range(3):
                total = total + r2[k, d, r, :].astype(F32)
            tot[k, i] = total
            square = total * total
            folded = square[:, :128]
            for t in range(1, WR // 128):
                folded = folded + square[:, t * 128 : (t + 1) * 128]
            sq[...] += folded[:8] + folded[8:]
        gsum[:, cols] = tot[k, mc]
        send(tot.at[k, 1 - mc], gsum.at[:, cols], tot_sem, 0, sibling)

    sq[...] = jnp.zeros_like(sq)
    def meet():
        pl.semaphore_wait(met_sem.at[0], 2)
        for peer in beside_x:
            signal(met_sem.at[1], peer)

    def pick_and_send(k):
        pick_rows(k)
        first_hops(k)

    for t in range(nr + sum(RS_LAG)):
        if t == RS_LAG[0]:
            meet()
        k = t
        for lag, stage in zip((0, *RS_LAG), (pick_and_send, second_hops, across, finish), strict=True):
            k -= lag
            if 0 <= k < nr:
                stage(k)

    mine_x, mine_yz = mx * 2 + mc, my * N + mz
    s1[mine_x] = sq[...]
    pl.semaphore_wait(met_sem.at[1], 2)
    for peer in peers_x:
        send(sq, s1.at[mine_x], x_sem, 0, peer)

    def flip(t, _):
        r = pl.ds(pl.multiple_of(t * 128, 128), 128)
        i = lax.broadcasted_iota(jnp.int32, (128, rows), 0) + t * 128
        eye = jnp.where(i == lax.broadcasted_iota(jnp.int32, (128, rows), 1), 1.0, 0.0).astype(BF16)
        perm_t[r, :] = lax.dot_general(
            eye, perm[...], (((1,), (1,)), ((), ())), preferred_element_type=F32
        ).astype(BF16)
        return 0

    lax.fori_loop(0, rows // 128, flip, 0)
    small[1].wait()
    small[2].wait()
    lane_row = lax.broadcasted_iota(jnp.int32, (16, WU), 0)
    count = jnp.zeros((16, WU), jnp.int32)
    for i in range(16):
        count = jnp.where(lane_row == i, steps[0, 0, i], count)
    count = count.astype(F32)
    fix[0] = 1.0 - jnp.power(jnp.full((16, WU), 0.9, F32), count)
    fix[1] = 1.0 - jnp.power(jnp.full((16, WU), 0.95, F32), count)
    for c in states:
        c.wait()

    for ref, sems in ((sib, pair_sem), (hop, hop_sem), (fin, fin_sem), (r2, r2_sem)):
        wait(ref, sems.at[0])

    few = s1.at[pl.ds(0, len(peers_x))]
    many = s2nd.at[pl.ds(0, len(peers_yz))]
    wait(few, x_sem.at[1])
    part = s1[0]
    for i in range(1, 2 * N):
        part = part + s1[i]
    s2nd[mine_yz] = part
    mine = s2nd.at[mine_yz]
    for peer in peers_yz:
        send(mine, mine, yz_sem, 0, peer)
    given = gsum.at[:, pl.ds(0, half)]
    wait(few, x_sem.at[0])
    wait(given, tot_sem.at[0])
    wait(given, tot_sem.at[1])
    wait(many, yz_sem.at[1])
    part = s2nd[0]
    for i in range(1, N * N):
        part = part + s2nd[i]
    square_sum = jnp.sum(jnp.sum(part, axis=1, keepdims=True), axis=0, keepdims=True)
    clip = jnp.minimum(1.0, max_rms[0] / jnp.sqrt(square_sum / entries + 1e-06))

    def update(k):
        def body(t, _):
            cols = pl.ds(pl.multiple_of(k * WG + t * WU, WU), WU)
            clipped = clip * gsum[:, cols]
            moment = 0.9 * st[1, :, cols] + 0.1 * clipped
            variance = 0.95 * st[2, :, cols] + 0.05 * clipped * clipped
            ratio = moment / fix[0] / (jnp.sqrt(variance / fix[1]) + 1e-08)
            old = st[0, :, cols]
            fresh = old - 0.1 * (ratio + 0.1 * old)
            new_master[0, 0, :, cols] = fresh
            new_first[0, 0, :, cols] = moment
            new_second[0, 0, :, cols] = variance
            slots[my, mz, mc, :, cols] = fresh.astype(BF16)
            return 0

        lax.fori_loop(0, WG // WU, body, 0)
        cols = pl.ds(k * WG, WG)
        a = axes(k)[0]
        mine = slots.at[my, mz, mc, :, cols]
        for d in (2, 1, 3):
            send(mine, mine, p1_sem, k, at[a][d])

    def row(k, at, part):
        cols = pl.ds(k * WG, WG)
        if k % 2 == 0:
            return slots.at[part, at, mc, :, cols]
        return slots.at[at, part, mc, :, cols]

    def spread(k):
        b = axes(k)[1]
        wait(slots.at[0, pl.ds(0, 3), 0, :, pl.ds(k * WG, WG)], p1_sem.at[1 + k])
        mine = row(k, coords[b], pl.ds(0, N))
        for d in (1, 3):
            send(mine, mine, p2_sem, k, at[b][d])

    def forward(k):
        b = axes(k)[1]
        wait(slots.at[pl.ds(0, 2), :, 0, :, pl.ds(k * WG, WG)], p2_sem.at[1 + k])
        for d, part in ((1, lo), (3, hi)):
            block = row(k, ring[b][4 - d], part)
            send(block, block, fwd_sem, k, at[b][d])

    def to_sibling(k):
        wait(slots.at[0, :, 0, :, pl.ds(k * WG, WG)], fwd_sem.at[1 + k])
        block = slots.at[:, :, mc, :, pl.ds(k * WG, WG)]
        send(block, block, half_sem, k, sibling)

    def put_back(k):
        wait(slots.at[:, :, 0, :, pl.ds(k * WG, WG)], half_sem.at[1 + k])
        restore(slots, perm_t, out, k * WG, k * WG)

    for k in range(ng):
        update(k)
    for t in range(ng + sum(AG_LAG)):
        k = t
        for lag, stage in zip((0, *AG_LAG), (spread, forward, to_sibling, put_back), strict=True):
            k -= lag
            if 0 <= k < (ng - LATE if stage is put_back else ng):
                stage(k)
    for k in range(ng - LATE, ng):
        wait(slots.at[:, :, 0, :, pl.ds(k * WG, WG)], half_sem.at[1 + k])
    wait(many, yz_sem.at[0])
    wait(slots.at[0, pl.ds(0, 3), 0], p1_sem.at[0])
    wait(slots.at[pl.ds(0, 2), :, 0], p2_sem.at[0])
    wait(slots.at[0, :, 0], fwd_sem.at[0])
    wait(slots.at[:, :, 0], half_sem.at[0])


def write_kernel(ready, m0, m1, m2, slots, perm_t, out, o0, o1, o2, tail, sem):
    first = ready.shape[1]
    copies = [
        pltpu.make_async_copy(src, dst, sem.at[i])
        for i, (src, dst) in enumerate(((ready, out.at[:, pl.ds(0, first)]), (m0, o0), (m1, o1), (m2, o2)))
    ]
    for c in copies:
        c.start()
    for k in range(LATE):
        restore(slots, perm_t, tail, first + k * WG, k * WG)
        part = pltpu.make_async_copy(
            tail.at[:, pl.ds(k * WG, WG)], out.at[:, pl.ds(first + k * WG, WG)], sem.at[4 + k]
        )
        part.start()
        copies.append(part)
    for c in copies:
        c.wait()


def shards(grad_parts, bucket_order, master, first_moment, second_moment, step_count, max_rms):
    _, rows, width = grad_parts.shape
    own_rows = master.shape[2]
    nr, ng = width // 2 // WR, width // WG
    entries = float(rows * width * lax.axis_size("x"))
    dma = pltpu.SemaphoreType.DMA
    vmem = pl.BlockSpec(memory_space=pltpu.VMEM)
    state = pltpu.VMEM(master.shape, F32)
    results = pl.pallas_call(
        functools.partial(main_kernel, (rows, width, nr, ng, entries)),
        out_shape=(
            pltpu.VMEM((rows, width - LATE * WG), BF16),
            state,
            state,
            state,
            pltpu.VMEM((N, N, 2, own_rows, width), BF16),
            pltpu.VMEM((rows, rows), BF16),
        ),
        in_specs=[pl.BlockSpec(memory_space=pltpu.HBM)] * 7,
        out_specs=[vmem] * 6,
        scratch_shapes=[
            pltpu.VMEM((nr, rows, WR), BF16),
            pltpu.VMEM((nr, rows, WR), BF16),
            pltpu.VMEM((nr, N, N, 32, WR), BF16),
            pltpu.VMEM((nr, 2, 2, 32, WR), BF16),
            pltpu.VMEM((nr, 2, N, 32, WR), BF16),
            pltpu.VMEM((nr, 3, 32, WR), BF16),
            pltpu.VMEM((nr, 3, 32, WR), BF16),
            pltpu.VMEM((nr, 2, 16, WR), F32),
            pltpu.VMEM((own_rows, width), F32),
            pltpu.VMEM((rows, rows), BF16),
            pltpu.VMEM((3, own_rows, width), F32),
            pltpu.VMEM((2, own_rows, WU), F32),
            pltpu.VMEM((8, 128), F32),
            pltpu.VMEM((2 * N, 8, 128), F32),
            pltpu.VMEM((N * N, 8, 128), F32),
            pltpu.SMEM(bucket_order.shape, jnp.int32),
            pltpu.SMEM(step_count.shape, jnp.int32),
            pltpu.SMEM(max_rms.shape, F32),
            dma((nr,)),
            *[dma((1 + nr,))] * 4,
            dma((2,)),
            dma((3,)),
            *[dma((2,))] * 2,
            *[dma((1 + ng,))] * 4,
            dma((3,)),
            pltpu.SemaphoreType.REGULAR((2,)),
        ],
        compiler_params=pltpu.CompilerParams(
            collective_id=0, has_side_effects=True, vmem_limit_bytes=48 << 20
        ),
    )(bucket_order, step_count, max_rms, grad_parts, master, first_moment, second_moment)
    fresh, *moved = pl.pallas_call(
        write_kernel,
        out_shape=[
            jax.ShapeDtypeStruct((rows, width), BF16),
            *[jax.ShapeDtypeStruct(master.shape, F32)] * 3,
        ],
        in_specs=[vmem] * 6,
        out_specs=[pl.BlockSpec(memory_space=pltpu.HBM)] * 4,
        scratch_shapes=[pltpu.VMEM((rows, LATE * WG), BF16), dma((4 + LATE,))],
        compiler_params=pltpu.CompilerParams(vmem_limit_bytes=12 << 20),
    )(*(pltpu.with_memory_space_constraint(r, pltpu.VMEM) for r in results))
    return (*moved, fresh)


def solution(mesh):
    dp = ("y", "z", "c")
    finer = Mesh(mesh.devices.reshape(N, N, 2, mesh.shape["expert"]), (*dp, "x"))
    state = P("x", dp, None, None)
    return jax.shard_map(
        shards,
        mesh=finer,
        in_specs=(P(dp, "x", None), P(), state, state, state, P("x", dp, None), P()),
        out_specs=(state, state, state, P("x", None)),
        check_vma=False,
    )
```
